32 devices in a mesh: docs: 8 (over z, x), ty: 2 (over y), tx: 2 (over core).
Axes of the slice: x: 2, y: 2, z: 4, core: 2. Of those that a mesh axis runs over, the one named last changes fastest.
Arguments:
- text_rows: float32 [24, 128, 4, 768], P('docs', None, ('ty', 'tx')), may hold values from -6 to 6
- patch_rows: float32 [24, 14, 14, 768], P('docs', 'ty', 'tx'), may hold values from -6 to 6
- text_boxes: int32 [24, 2, 512], P('docs'), may hold values from 0 to 127
- lengths: int32 [24], P('docs'), may hold values from 1 to 512, 6144 in all
- project_weight: float32 [768, 2304], replicated, may hold values from -0.21875 to 0.21875
- query_bias: float32 [768], replicated, may hold values from -3 to 3
- value_bias: float32 [768], replicated, may hold values from -3 to 3
- out_weight: float32 [768, 768], replicated, may hold values from -1.75 to 1.75
- out_bias: float32 [768], replicated, may hold values from -3 to 3
- gain_one: float32 [768], replicated, may hold values from 0.5 to 1.5
- shift_one: float32 [768], replicated, may hold values from -3 to 3
- up_weight: float32 [768, 3072], replicated, may hold values from -0.21875 to 0.21875
- up_bias: float32 [3072], replicated, may hold values from -3 to 3
- down_weight: float32 [3072, 768], replicated, may hold values from -0.109375 to 0.109375
- down_bias: float32 [768], replicated, may hold values from -3 to 3
- gain_two: float32 [768], replicated, may hold values from 0.5 to 1.5
- shift_two: float32 [768], replicated, may hold values from -3 to 3
- bucket_bias: float32 [1536], replicated, may hold values from -4 to 4
- text_cotangent: float32 [24, 128, 4, 768], P('docs', None, ('ty', 'tx')), may hold values from -6 to 6
- patch_cotangent: float32 [24, 14, 14, 768], P('docs', 'ty', 'tx'), may hold values from -6 to 6
Outputs:
- text_output: float32 [24, 128, 4, 768], P('docs', None, ('ty', 'tx'))
- patch_output: float32 [24, 14, 14, 768], P('docs', 'ty', 'tx')
- text_gradient: float32 [24, 128, 4, 768], P('docs', None, ('ty', 'tx'))
- patch_gradient: float32 [24, 14, 14, 768], P('docs', 'ty', 'tx')
- project_gradient: float32 [768, 2304], P(None, 'docs')
- query_bias_gradient: float32 [768], P('docs')
- value_bias_gradient: float32 [768], P('docs')
- out_weight_gradient: float32 [768, 768], P(None, 'docs')
- out_bias_gradient: float32 [768], P('docs')
- gain_one_gradient: float32 [768], P('docs')
- shift_one_gradient: float32 [768], P('docs')
- up_weight_gradient: float32 [768, 3072], P(None, 'docs')
- up_bias_gradient: float32 [3072], P('docs')
- down_weight_gradient: float32 [3072, 768], P(None, 'docs')
- down_bias_gradient: float32 [768], P('docs')
- gain_two_gradient: float32 [768], P('docs')
- shift_two_gradient: float32 [768], P('docs')
- bucket_bias_gradient: float32 [1536], P('docs')
The draws below stay inside these ranges and needn't reach their ends.
Inputs may be any that keep to these rules, and one draw needn't show every extreme that they name: `lengths`: some document has exactly 512 live text positions.
All inputs are finite; a program needn't handle non-finite values. No bound on the sum of `lengths` on one device may be relied on, other than what follows from the above.
Results may differ from the reference program's by a relative error of at most 0.018.
Values may be sent and summed in bfloat16 or wider, within the bound.
No kernel may reach another device: no remote copies, remote signals or barrier semaphores. Data moves between devices by JAX's collectives and lax.ppermute only.
A program may use at most 256 MiB of HBM per device.

```python
import math
from functools import partial
import jax
import jax.numpy as jnp
import numpy as np
from jax import lax

D = 768
H = 12
DH = 64
FF = 3072
BUCKETS = 64
LEVELS = 128
GRID = 14
HW = 3
TT = 128
DOCS = 24
TILES = 4
TILE = 7
TEXT = 512
N_TX = 2


def place_ends(values, own_key, low, high):
    longest = values.shape.index(max(values.shape))
    spots = []
    for shift in (0, 1):
        where = [jax.random.randint(jax.random.fold_in(own_key, axis), (), 0, length) for axis, length in enumerate(values.shape)]
        where[longest] = (where[longest] + shift) % values.shape[longest]
        spots.append(tuple(where))
    return values.at[spots[0]].set(low).at[spots[1]].set(high)


def raised(drawn, stream_key, source, target, parts, factor):
    def block_of(axis_at):
        return (jnp.arange(drawn.shape[axis_at]) // (drawn.shape[axis_at] // parts)).reshape((-1,) + (1,) * (drawn.ndim - 1 - axis_at))

    first = jax.random.permutation(stream_key, parts)[block_of(target)]
    second = (block_of(target) + parts // 2) % parts
    return jnp.where((block_of(source) == first) | (block_of(source) == second), factor * drawn, drawn)


def steps_of(rng, shape, split, low, largest):
    def one(position, parts):
        heights = jax.random.uniform(jax.random.fold_in(jax.random.fold_in(rng, 6), position), (parts,), jnp.float32, low / len(split), largest / len(split))
        return jnp.repeat(jnp.exp(heights), shape[position] // parts).reshape((-1,) + (1,) * (len(shape) - position - 1))

    loudness = one(*split[0])
    for cut in split[1:]:
        loudness = loudness * one(*cut)
    return loudness


def split_up(amount, total, reach, skew):
    portions = [(1 << 20) // math.isqrt(grade ** skew) + 1 for grade in range(2, amount + 1)]
    surplus, counts = total - reach - (amount - 1), [1] * (amount - 1)
    while surplus > 0:
        candidates = [i for i in range(amount - 1) if counts[i] < reach]
        mass, remaining = sum([portions[i] for i in candidates]), surplus
        for i in candidates:
            more = min(reach - counts[i], max(1, remaining * portions[i] // mass), surplus)
            counts[i] = counts[i] + more
            surplus = surplus - more
    return np.array([reach] + counts)


def uneven(own_key, number_of, total, bound, skew):
    if number_of == 2:
        one = jax.random.randint(own_key, (), max(1, total - bound), min(bound, total - 1) + 1)
        return jnp.stack([one, total - one])
    sizes = jnp.asarray(split_up(number_of, total, bound, skew), jnp.int32)
    couples = (number_of - 1) // 2
    giver, receiver = sizes[1:1 + 2 * couples:2], sizes[2:2 + 2 * couples:2]
    room = jnp.minimum(giver - 1, bound - receiver)
    moved = jax.random.randint(jax.random.fold_in(own_key, 1), (couples,), 0, 1 << 20) % (room + 1)
    sizes = sizes.at[1:1 + 2 * couples:2].set(giver - moved).at[2:2 + 2 * couples:2].set(receiver + moved)
    return sizes[jax.random.permutation(jax.random.fold_in(own_key, 2), number_of)]


def bell_draw(own_key, dims, deviation, most, split=(), kind=jnp.bfloat16):
    level = steps_of(own_key, dims, split, -0.22, 0.18) if split else 1.0
    drawn = jax.random.normal(own_key, dims, jnp.float32) * deviation * level
    return jnp.minimum(jnp.maximum(drawn, -most), most).astype(kind)


def gaussian_with(own_key, dims, spread, reach, split, heavy, kind=jnp.bfloat16):
    values = spread * jax.random.normal(own_key, dims, jnp.float32)
    if split:
        values = values * steps_of(own_key, dims, split, -0.22, 0.18)
    return jnp.clip(raised(values, jax.random.fold_in(own_key, 3), *heavy), -reach, reach).astype(kind)


def setup_inputs(seed: int = 0) -> dict:
    seeds = jax.random.split(jax.random.key(seed), 21)
    text_rows = bell_draw(seeds[0], (DOCS, TT, TILES, D), 1.0, 6.0, ((0, 8), (2, 4)), jnp.float32)
    patch_rows = bell_draw(seeds[1], (DOCS, GRID, GRID, D), 1.0, 6.0, ((0, 8), (1, 2), (2, 2)), jnp.float32)
    text_boxes = place_ends(jax.random.randint(seeds[2], (DOCS, 2, TEXT), 0, LEVELS), jax.random.fold_in(seeds[2], 1), 0, LEVELS - 1).astype(jnp.int32)
    lengths = uneven(seeds[3], DOCS, 2 * TT * DOCS, TEXT, 2).astype(jnp.int32)
    project_weight = bell_draw(seeds[4], (D, 3 * D), D ** -0.5, 0.21875, (), jnp.float32)
    query_bias = bell_draw(seeds[5], (D,), 0.5, 3.0, (), jnp.float32)
    value_bias = bell_draw(seeds[6], (D,), 0.5, 3.0, (), jnp.float32)
    out_weight = bell_draw(seeds[7], (D, D), (D // 64) ** -0.5, 1.75, (), jnp.float32)
    out_bias = bell_draw(seeds[8], (D,), 0.5, 3.0, (), jnp.float32)
    gain_one = jnp.clip(1.0 + 0.1 * jax.random.normal(seeds[9], (D,), jnp.float32), 0.5, 1.5)
    shift_one = bell_draw(seeds[10], (D,), 0.5, 3.0, (), jnp.float32)
    up_weight = bell_draw(seeds[11], (D, FF), D ** -0.5, 0.21875, (), jnp.float32)
    up_bias = bell_draw(seeds[12], (FF,), 0.5, 3.0, (), jnp.float32)
    down_weight = bell_draw(seeds[13], (FF, D), FF ** -0.5, 0.109375, (), jnp.float32)
    down_bias = bell_draw(seeds[14], (D,), 0.5, 3.0, (), jnp.float32)
    gain_two = jnp.clip(1.0 + 0.1 * jax.random.normal(seeds[15], (D,), jnp.float32), 0.5, 1.5)
    shift_two = bell_draw(seeds[16], (D,), 0.5, 3.0, (), jnp.float32)
    bucket_bias = bell_draw(seeds[17], (2 * H * BUCKETS,), 1.0, 4.0, (), jnp.float32)
    text_cotangent = gaussian_with(seeds[18], (DOCS, TT, TILES, D), 1.0, 6.0, ((0, 8), (2, 4)), (0, 3, 8, 2.0), jnp.float32)
    patch_cotangent = gaussian_with(seeds[19], (DOCS, GRID, GRID, D), 1.0, 6.0, ((0, 8), (1, 2), (2, 2)), (0, 3, 8, 2.0), jnp.float32)
    return {"text_rows": text_rows, "patch_rows": patch_rows, "text_boxes": text_boxes, "lengths": lengths, "project_weight": project_weight, "query_bias": query_bias, "value_bias": value_bias, "out_weight": out_weight, "out_bias": out_bias, "gain_one": gain_one, "shift_one": shift_one, "up_weight": up_weight, "up_bias": up_bias, "down_weight": down_weight, "down_bias": down_bias, "gain_two": gain_two, "shift_two": shift_two, "bucket_bias": bucket_bias, "text_cotangent": text_cotangent, "patch_cotangent": patch_cotangent}


@jax.custom_vjp
def low(v):
    return lax.optimization_barrier(v.astype(jnp.bfloat16)).astype(jnp.float32)

@jax.custom_vjp
def low_back(v):
    return v

def low_keep(v):
    return (low(v), None)

def low_pass(kept, grad):
    return (grad,)

def back_keep(v):
    return (v, None)

def back_low(kept, grad):
    return (low(grad),)
low.defvjp(low_keep, low_pass)
low_back.defvjp(back_keep, back_low)
HIGHEST = lax.Precision.HIGHEST

def product(left, right):
    return jnp.dot(left, right, precision=HIGHEST, preferred_element_type=jnp.float32)

def layer_norm(values, gain, shift):
    center = values - lax.optimization_barrier(jnp.mean(values, axis=-1, keepdims=True))
    return center * lax.rsqrt(lax.optimization_barrier(jnp.mean(center * center, axis=-1, keepdims=True)) + 1e-05) * gain + shift

def patch_level(cell_index):
    return ((2 * cell_index + 1) * LEVELS // (2 * GRID)).astype(jnp.int32)

def document_layer(params, tokens, length, text_boxes):
    project_weight, query_bias, value_bias, out_weight, out_bias, gain_one, shift_one, up_weight, up_bias, down_weight, down_bias, gain_two, shift_two, bucket_bias = params
    token_count = tokens.shape[0]
    positions = jnp.arange(TEXT, dtype=jnp.int32)
    text_live = positions < length
    text_tile = positions % TILES
    cells = jnp.arange(GRID * GRID, dtype=jnp.int32)
    cell_row = cells // GRID
    cell_col = cells % GRID
    row_start = jnp.concatenate([text_tile // N_TX, cell_row // TILE]) * TILE - HW
    col_start = jnp.concatenate([text_tile % N_TX, cell_col // TILE]) * TILE - HW
    near = (cell_row[None, :] >= row_start[:, None]) & (cell_row[None, :] < row_start[:, None] + TILE + 2 * HW) & (cell_col[None, :] >= col_start[:, None]) & (cell_col[None, :] < col_start[:, None] + TILE + 2 * HW)
    allowed = jnp.concatenate([jnp.broadcast_to(text_live[None, :], (token_count, TEXT)), near], axis=1)
    query_live = jnp.concatenate([text_live, jnp.ones((GRID * GRID,), jnp.bool_)])
    coord_x = jnp.concatenate([text_boxes[0].astype(jnp.int32), patch_level(cell_col)])
    coord_y = jnp.concatenate([text_boxes[1].astype(jnp.int32), patch_level(cell_row)])
    half_span = BUCKETS // 2
    index_x = jnp.clip(coord_x[:, None] - coord_x[None, :], -half_span, half_span - 1) + half_span
    index_y = jnp.clip(coord_y[:, None] - coord_y[None, :], -half_span, half_span - 1) + half_span
    table = bucket_bias.reshape(2, H, BUCKETS)
    pair_bias = table[0][:, index_x] + table[1][:, index_y]
    token_low = low(tokens)
    mixture = product(token_low, low(project_weight))
    queries = low_back(low((mixture[:, :D] + query_bias) * 0.125)).reshape(token_count, H, DH)
    key_heads = low_back(low(mixture[:, D:2 * D])).reshape(token_count, H, DH)
    value_heads = low_back(low(mixture[:, 2 * D:] + value_bias)).reshape(token_count, H, DH)
    scores = low_back(jnp.einsum('qhd,khd->hqk', queries, key_heads, precision=HIGHEST) + pair_bias)
    scores = jnp.where(allowed[None], scores, -1e+30)
    weights = low(jax.nn.softmax(scores, axis=-1))
    attended = jnp.einsum('hqk,khd->qhd', weights, value_heads, precision=HIGHEST).reshape(token_count, D)
    attended = low_back(low(attended))
    branch = low_back(product(attended, low(out_weight)) + out_bias)
    normed = layer_norm(tokens + branch, gain_one, shift_one)
    pre_up = low_back(product(low(normed), low(up_weight)) + up_bias)
    activated = low(jax.nn.gelu(pre_up, approximate=False))
    feed = low_back(product(activated, low(down_weight)) + down_bias)
    return layer_norm(normed + feed, gain_two, shift_two) * query_live[:, None]

def forward(text_rows, patch_rows, params, lengths, text_boxes):
    row_total = TEXT + GRID * GRID
    tokens = jnp.concatenate([text_rows.reshape(DOCS, TEXT, D), patch_rows.reshape(DOCS, GRID * GRID, D)], axis=1)
    groups = DOCS // 4

    def group_layer(items):
        return jax.vmap(partial(document_layer, params))(items[0], items[1], items[2])
    result = lax.map(jax.checkpoint(group_layer), (tokens.reshape(groups, 4, row_total, D), lengths.reshape(groups, 4), text_boxes.reshape(groups, 4, 2, TEXT)))
    result = result.reshape(DOCS, row_total, D)
    return (result[:, :TEXT].reshape(DOCS, TT, TILES, D), result[:, TEXT:].reshape(DOCS, GRID, GRID, D))

def reference(text_rows, patch_rows, text_boxes, lengths, project_weight, query_bias, value_bias, out_weight, out_bias, gain_one, shift_one, up_weight, up_bias, down_weight, down_bias, gain_two, shift_two, bucket_bias, text_cotangent, patch_cotangent):
    params = (project_weight, query_bias, value_bias, out_weight, out_bias, gain_one, shift_one, up_weight, up_bias, down_weight, down_bias, gain_two, shift_two, bucket_bias)

    def closed(text_part, patch_part, param_part):
        return forward(text_part, patch_part, param_part, lengths, text_boxes)
    outputs, pullback = jax.vjp(closed, text_rows, patch_rows, params)
    text_gradient, patch_gradient, grads = pullback((text_cotangent, patch_cotangent))
    return (outputs[0], outputs[1], text_gradient, patch_gradient, grads[0], grads[1], grads[2], grads[3], grads[4], grads[5], grads[6], grads[7], grads[8], grads[9], grads[10], grads[11], grads[12], grads[13])
```

```python
import functools

import jax
import jax.numpy as jnp
from jax import lax
from jax.experimental import pallas as pl
from jax.experimental.pallas import tpu as pltpu
from jax.sharding import PartitionSpec as P

D = 768
H = 12
DH = 64
FF = 3072
BUCKETS = 64
LEVELS = 128
GRID = 14
HW = 3
TT = 128

EPSILON = 1e-05
HIGHEST = lax.Precision.HIGHEST
SIDE = 7
CELLS = SIDE * SIDE
ROWS = 192
SLOT = ROWS - TT
WIN = SIDE + HW
KEYS = 640
GROUPS = 3
GH = H // GROUPS
GW = GH * DH
CHUNKS = 6
FC = FF // CHUNKS
HALF = D // 2
BF = jnp.bfloat16
F32 = jnp.float32
NEG = -1e30


def dot(a, b, ca=1, cb=0, precision=None):
    return lax.dot_general(
        a, b, (((ca,), (cb,)), ((), ())), preferred_element_type=F32, precision=precision
    )


def call(kernel, grid, ins, outs, shapes, scratch=(), prefetch=1, cost=(0, 0)):
    return pl.pallas_call(
        kernel,
        grid_spec=pltpu.PrefetchScalarGridSpec(
            num_scalar_prefetch=prefetch,
            grid=grid,
            in_specs=ins,
            out_specs=outs,
            scratch_shapes=list(scratch),
        ),
        out_shape=shapes,
        compiler_params=pltpu.CompilerParams(
            dimension_semantics=("arbitrary",) * len(grid), vmem_limit_bytes=60 << 20
        ),
        cost_estimate=pl.CostEstimate(flops=cost[0], bytes_accessed=cost[1], transcendentals=0),
    )


def whole(shape):
    return pl.BlockSpec(shape, lambda *_: (0,) * len(shape))


def shape(dims, dtype):
    return jax.ShapeDtypeStruct(dims, dtype)


def put_rows(dst, base, text, patch, cast):
    dst[base : base + TT] = cast(text)
    for i in range(SIDE):
        dst[base + TT + SIDE * i : base + TT + SIDE * (i + 1)] = cast(patch[i])
    dst[base + TT + CELLS : base + ROWS] = jnp.zeros((SLOT - CELLS, D), dst.dtype)


def rows_kernel(text, patch, low, buf):
    put_rows(buf, 0, text[0], patch[0], lambda v: v)
    low[0] = buf[...].astype(BF)


def forward_kernel(
    own, core, side, diag, pick, wq, wk, wv, qb, vb, key_hot, mask, query_hot, ramp,
    keys_out, q_out, k_out, v_out, mix_out, lse_out, bias_out, keys, table,
):
    g = pl.program_id(0)
    d = pl.program_id(1)

    @pl.when(g == 0)
    def _():
        tiles = (own, core, side, diag)
        for c in range(4):
            for r in range(4):
                at = c * 128 + r * 32
                keys[d, at : at + 32] = tiles[r][0, c * 32 : c * 32 + 32]
        cells = jnp.concatenate([t[0, TT:] for t in tiles], axis=0)
        keys[d, 512:KEYS] = dot(pick[...], cells).astype(BF)

    @pl.when(g == 0)
    def _():
        keys_out[0] = keys[d]

    @pl.when(d == 0)
    def _():
        for h in range(GH):
            for s in range(2):
                line = jnp.broadcast_to(ramp[0, s * GH + h : s * GH + h + 1], (LEVELS, 256))
                rolled = pltpu.roll(line, 0, 1, stride=1, stride_axis=0)
                table[h, :, s * LEVELS : (s + 1) * LEVELS] = rolled[:, :LEVELS].astype(BF)

    rows = keys[d]
    key4 = dot(rows, wk[...]).astype(BF)
    value4 = (dot(rows, wv[...]) + vb[...]).astype(BF)
    query4 = ((dot(own[0], wq[...]) + qb[...]) * 0.125).astype(BF)
    k_out[0] = key4
    v_out[0] = value4
    q_out[0] = query4
    lane = lax.broadcasted_iota(jnp.int32, (ROWS, 128), 1)
    hot = query_hot[0]
    logs = jnp.zeros((ROWS, 128), F32)
    for p in range(2):
        cut = slice(128 * p, 128 * (p + 1))
        pieces = []
        for half in range(2):
            h = 2 * p + half
            mine = (lane < DH) if half == 0 else (lane >= DH)
            masked = jnp.where(mine, query4[:, cut], jnp.zeros((), BF))
            tab = table[h]
            shift = jnp.concatenate(
                [
                    dot(hot[:, :LEVELS], tab[:, :LEVELS]).astype(BF),
                    dot(hot[:, LEVELS:], tab[:, LEVELS:]).astype(BF),
                ],
                axis=1,
            )
            bias_out[0, h] = shift
            score = dot(masked, key4[:, cut], 1, 1) + dot(shift, key_hot[0]) + mask[0]
            top = jnp.max(score, axis=1, keepdims=True)
            power = jnp.exp(score - top)
            total = jnp.sum(power, axis=1, keepdims=True)
            mixed = dot(power.astype(BF), value4[:, cut]) / total
            pieces.append(mixed)
            logs = jnp.where(lane == h, top + jnp.log(total), logs)
        mix_out[0, :, cut] = jnp.where(lane < DH, pieces[0], pieces[1]).astype(BF)
    lse_out[0, 0] = jnp.transpose(logs)[:8]


def stats(v):
    center = v - jnp.mean(v, axis=-1, keepdims=True)
    inv = lax.rsqrt(jnp.mean(center * center, axis=-1, keepdims=True) + EPSILON)
    return center * inv, inv


def back_norm(grad, normed, inv):
    return inv * (
        grad
        - jnp.mean(grad, axis=-1, keepdims=True)
        - normed * jnp.mean(grad * normed, axis=-1, keepdims=True)
    )


def feed_kernel(
    info, mix, text, patch, text_cot, patch_cot, wo, wu, wd, bo, g1, s1, bu, bd, g2, s2,
    norm_out, inv_out, low_out, slope_out, text_out, patch_out, dz_out, df_out, vec_out,
    keep_out, send_out, buf, hidden, low, feed, active, df,
):
    i = pl.program_id(0)
    docs = text.shape[0]
    total = docs * ROWS

    @pl.when(i == 0)
    def _():
        for d in range(docs):
            put_rows(buf, d * ROWS, text[d], patch[d], lambda v: v)
        normed, inv = stats(buf[...] + (dot(mix[...], wo[...]) + bo[...]))
        norm_out[...] = normed
        inv_out[...] = jnp.broadcast_to(inv, (total, 128))
        out = normed * g1[...] + s1[...]
        hidden[...] = out
        low[...] = out.astype(BF)
        low_out[...] = out.astype(BF)
        feed[...] = jnp.zeros_like(feed)

    @pl.when(i < CHUNKS)
    def _():
        u = dot(low[...], wu[...]) + bu[...]
        phi = 0.5 * (1.0 + lax.erf(u * 0.7071067811865476))
        slope_out[...] = phi + u * (0.3989422804014327 * jnp.exp(-0.5 * u * u))
        act = (u * phi).astype(BF)
        active[i] = act
        feed[...] += dot(act, wd[...])

    @pl.when(i == CHUNKS - 1)
    def _():
        normed, inv = stats(hidden[...] + (feed[...] + bd[...]))
        row = lax.broadcasted_iota(jnp.int32, (total, 1), 0)
        live = jnp.zeros((total, 1), F32)
        for d in range(docs):
            at = row - d * ROWS
            ok = (at >= 0) & (at < ROWS) & ((at >= TT) | (4 * at + info[1] < info[2 + d]))
            live = jnp.where(ok, 1.0, live)
        feed[...] = (normed * g2[...] + s2[...]) * live
        for d in range(docs):
            base = d * ROWS
            text_out[d] = feed[base : base + TT]
            for k in range(SIDE):
                at = base + TT + SIDE * k
                patch_out[d, k] = feed[at : at + SIDE]
        for d in range(docs):
            put_rows(buf, d * ROWS, text_cot[d], patch_cot[d], lambda v: v)
        cot = buf[...] * live
        vec_out[0:1] = jnp.sum(cot * normed, axis=0, keepdims=True)
        vec_out[1:2] = jnp.sum(cot, axis=0, keepdims=True)
        dz = back_norm(cot * g2[...], normed, inv)
        dz_out[...] = dz
        df[...] = dz.astype(BF)
        df_out[...] = dz.astype(BF)
        vec_out[2:3] = jnp.sum(dz.astype(BF).astype(F32), axis=0, keepdims=True)
        vec_out[3:8] = jnp.zeros((5, D), F32)

    k = i - CHUNKS
    half = CHUNKS // 2

    @pl.when((i >= CHUNKS) & (k < half))
    def _():
        keep_out[...] = dot(df[...], active[half * info[0] + k], 0, 0).astype(BF)

    @pl.when((i >= CHUNKS) & (k >= half))
    def _():
        send_out[...] = dot(df[...], active[half * (1 - info[0]) + k - half], 0, 0).astype(BF)


def feed_back_kernel(
    info, df, dz, slope, low, normed, inv, mix, wo, wu, wd, g1,
    bu_out, vec_out, dh_out, do_out, up_keep, up_send, out_keep, out_send, acc,
):
    i = pl.program_id(0)
    first = info[0] == 0

    @pl.when(i == 0)
    def _():
        acc[...] = dz[...]

    du32 = dot(df[...], wd[...], 1, 1) * slope[...]
    du = du32.astype(BF)
    bu_out[...] = jnp.sum(du.astype(F32), axis=0, keepdims=True)
    acc[...] += dot(du, wu[...], 1, 1)
    grad = dot(du, low[...], 0, 0)
    up_keep[...] = jnp.where(first, grad[:, :HALF], grad[:, HALF:]).astype(BF)
    up_send[...] = jnp.where(first, grad[:, HALF:], grad[:, :HALF]).astype(BF)

    @pl.when(i == CHUNKS - 1)
    def _():
        dy = acc[...]
        n1 = normed[...]
        vec_out[0:1] = jnp.sum(dy * n1, axis=0, keepdims=True)
        vec_out[1:2] = jnp.sum(dy, axis=0, keepdims=True)
        dh = back_norm(dy * g1[...], n1, inv[:, 0:1])
        dh_out[...] = dh
        da = dh.astype(BF)
        vec_out[2:3] = jnp.sum(da.astype(F32), axis=0, keepdims=True)
        vec_out[3:8] = jnp.zeros((5, D), F32)
        do_out[...] = dot(da, wo[...], 1, 1).astype(BF)
        grad = dot(da, mix[...], 0, 0)
        out_keep[...] = jnp.where(first, grad[:, :HALF], grad[:, HALF:]).astype(BF)
        out_send[...] = jnp.where(first, grad[:, HALF:], grad[:, :HALF]).astype(BF)


def backward_kernel(
    info, keys, own, q, k, v, mix, do, lse, bias, key_hot, hot_rows, flip_hot, mask,
    dq_out, dk_out, dv_out, keep_out, send_out, qb_out, vb_out, bucket_out, acc, maps, sums,
):
    d = pl.program_id(1)
    last = pl.num_programs(1) - 1
    first = info[0] == 0

    @pl.when(d == 0)
    def _():
        acc[...] = jnp.zeros_like(acc)
        maps[...] = jnp.zeros_like(maps)
        sums[...] = jnp.zeros_like(sums)

    lane = lax.broadcasted_iota(jnp.int32, (ROWS, 128), 1)
    head = lax.broadcasted_iota(jnp.int32, (8, GW), 0)
    span = lax.broadcasted_iota(jnp.int32, (8, GW), 1) // DH
    pick = (head == span).astype(F32)
    do4 = do[0]
    q4 = q[0]
    delta = dot(pick, do4.astype(F32) * mix[0].astype(F32), 1, 1, HIGHEST)
    zero = jnp.zeros((), BF)
    for p in range(2):
        cut = slice(128 * p, 128 * (p + 1))
        kp = k[0, :, cut]
        vp = v[0, :, cut]
        kt = jnp.transpose(kp)
        dk = jnp.zeros((KEYS, 128), F32)
        dv = jnp.zeros((KEYS, 128), F32)
        dq = []
        for half in range(2):
            h = 2 * p + half
            mine = (lane < DH) if half == 0 else (lane >= DH)
            qm = jnp.where(mine, q4[:, cut], zero)
            dm = jnp.where(mine, do4[:, cut], zero)
            score = dot(kp, qm, 1, 1) + dot(hot_rows[0], bias[0, h], 1, 1)
            prob = jnp.exp(score + (jnp.concatenate([mask[0], mask[0, :, :64]], axis=1) - lse[0, 0, h : h + 1]))
            grad = dot(vp, dm, 1, 1) - delta[h : h + 1]
            ds = (prob * grad).astype(BF)
            dv = dv + dot(prob.astype(BF), dm)
            dk = dk + dot(ds, qm)
            dq.append(dot(kt[DH * half : DH * (half + 1)], ds))
            by_key = dot(key_hot[0], ds).astype(BF)
            for s in range(2):
                maps[h, s] += dot(by_key[LEVELS * s : LEVELS * (s + 1)], flip_hot[0, :, LEVELS * s : LEVELS * (s + 1)])
        dk_out[0, :, cut] = dk.astype(BF)
        dv_out[0, :, cut] = dv.astype(BF)
        dq_out[0, :, cut] = jnp.transpose(jnp.concatenate(dq, axis=0)).astype(BF) * 0.125
    dq4 = dq_out[0]
    dk4 = dk_out[0]
    dv4 = dv_out[0]
    acc[0:GW] += dot(dq4, own[0], 0, 0)
    acc[GW : 2 * GW] += dot(dk4, keys[0], 0, 0)
    acc[2 * GW :] += dot(dv4, keys[0], 0, 0)
    sums[0:1] += jnp.sum(dq4.astype(F32), axis=0, keepdims=True)
    sums[1:2] += jnp.sum(dv4.astype(F32), axis=0, keepdims=True)

    @pl.when(d == last)
    def _():
        for s in range(3):
            grad = acc[s * GW : (s + 1) * GW]
            keep_out[s] = jnp.where(first, grad[:, :HALF], grad[:, HALF:]).astype(BF)
            send_out[s] = jnp.where(first, grad[:, HALF:], grad[:, :HALF]).astype(BF)
        qb_out[...] = sums[0:1]
        vb_out[...] = sums[1:2]
        at = lax.broadcasted_iota(jnp.int32, (256, BUCKETS), 0)
        bucket = jnp.clip(LEVELS - 1 - at, -(BUCKETS // 2), BUCKETS // 2 - 1) + BUCKETS // 2
        to_bucket = (bucket == lax.broadcasted_iota(jnp.int32, (256, BUCKETS), 1)).astype(F32)
        lines = []
        for s in range(2):
            for h in range(GH):
                wide = jnp.concatenate([maps[h, s], jnp.zeros((LEVELS, LEVELS), F32)], axis=1)
                lines.append(jnp.sum(pltpu.roll(wide, 0, 1, stride=1, stride_axis=0), axis=0, keepdims=True))
        bucket_out[0] = dot(jnp.concatenate(lines, axis=0), to_bucket, 1, 0, HIGHEST)


def input_kernel(dq, dk, dv, dh, pick, wq, wk, wv, own_out, cross_out, side_out, part):
    part[...] = dot(dk[0], wk[...], 1, 1) + dot(dv[0], wv[...], 1, 1)
    query = dot(dq[0], wq[...], 1, 1)
    cells = dot(pick[...], part[512:KEYS].astype(BF), 0, 0)

    def emit(r, store):
        for c in range(4):
            at = c * 128 + r * 32
            store(slice(c * 32, c * 32 + 32), part[at : at + 32])
        store(slice(TT, ROWS), cells[r * SLOT : (r + 1) * SLOT])

    def own_store(at, value):
        own_out[0, at] = dh[0, at] + (query[at] + value)

    def core_store(at, value):
        cross_out[0, 0, at] = value.astype(BF)

    def diag_store(at, value):
        cross_out[1, 0, at] = value.astype(BF)

    def side_store(at, value):
        side_out[0, at] = value.astype(BF)

    emit(0, own_store)
    emit(1, core_store)
    emit(2, side_store)
    emit(3, diag_store)


def final_kernel(own, cross, side, text_out, patch_out, buf):
    buf[...] = own[0] + cross[0, 0].astype(F32) + side[0].astype(F32)
    text_out[0] = buf[:TT]
    for i in range(SIDE):
        at = TT + SIDE * i
        patch_out[0, i] = buf[at : at + SIDE]


def patch_level(cell_index):
    return (2 * cell_index + 1) * LEVELS // (2 * GRID)


def swap(value, axis):
    return lax.ppermute(value, axis, [(0, 1), (1, 0)])


def exchange(value, axis, mask):
    count = lax.axis_size(axis)
    return lax.ppermute(value, axis, [(i, i ^ mask) for i in range(count)])


def added(a, b):
    return (a.astype(F32) + b.astype(F32)).astype(a.dtype)


def halves(value, bit, dim):
    keep = lax.dynamic_index_in_dim(value, bit, dim, keepdims=False)
    send = lax.dynamic_index_in_dim(value, 1 - bit, dim, keepdims=False)
    return keep, send


def docs_stages(value, lead):
    count = lax.axis_size("docs")
    bits = count.bit_length() - 1
    here = lax.axis_index("docs")
    for b in range(bits):
        dim = lead + bits - 1 - b
        keep, send = halves(value, (here >> b) & 1, dim)
        value = added(keep, exchange(send, "docs", 1 << b))
    return value


def tile_half(value, axis, bit):
    keep, send = halves(value, bit, axis)
    return added(keep, swap(send, "ty"))


def reduced(keep, send, rows, side_first):
    count = lax.axis_size("docs")
    bits = count.bit_length() - 1
    ty = lax.axis_index("ty")
    columns = keep.shape[-1]
    value = added(keep, swap(send, "tx"))
    value = value.reshape((2,) * bits + (2, rows // 2, columns))
    if side_first:
        value = tile_half(value, bits, ty)
        value = docs_stages(value, 0)
    else:
        value = docs_stages(value, 0)
        value = tile_half(value, 0, ty)
    return value


def joined(value, axis, dim):
    other = swap(value, axis)
    low = lax.axis_index(axis) == 0
    return jnp.concatenate(
        [jnp.where(low, value, other), jnp.where(low, other, value)], axis=dim
    )


def gathered(value):
    return joined(joined(value, "ty", 0), "tx", 1).astype(F32).T


def shards(
    text_rows,
    patch_rows,
    text_boxes,
    lengths,
    project_weight,
    query_bias,
    value_bias,
    out_weight,
    out_bias,
    gain_one,
    shift_one,
    up_weight,
    up_bias,
    down_weight,
    down_bias,
    gain_two,
    shift_two,
    bucket_bias,
    text_cotangent,
    patch_cotangent,
):
    docs = text_rows.shape[0]
    total = docs * ROWS
    tx = lax.axis_index("tx")
    ty = lax.axis_index("ty")
    own_tile = 2 * ty + tx
    info = jnp.concatenate([jnp.stack([tx, own_tile]).astype(jnp.int32), lengths])
    text = text_rows.reshape(docs, TT, D)
    text_cot = text_cotangent.reshape(docs, TT, D)

    low_rows = pl.pallas_call(
        rows_kernel,
        grid=(docs,),
        in_specs=[
            pl.BlockSpec((1, TT, D), lambda d: (d, 0, 0)),
            pl.BlockSpec((1, SIDE, SIDE, D), lambda d: (d, 0, 0, 0)),
        ],
        out_specs=pl.BlockSpec((1, ROWS, D), lambda d: (d, 0, 0)),
        out_shape=shape((docs, ROWS, D), BF),
        scratch_shapes=[pltpu.VMEM((ROWS, D), F32)],
    )(text, patch_rows)
    side_rows = swap(low_rows, "ty")
    core_rows = swap(low_rows, "tx")
    diag_rows = swap(side_rows, "tx")

    wp = project_weight.astype(BF)
    wo = out_weight.astype(BF)
    wu = up_weight.astype(BF)
    wd = down_weight.astype(BF)

    grid = text_boxes.reshape(docs, 2, TT, 2, 2)
    grid = jnp.where(ty == 1, grid[:, :, :, ::-1], grid)
    grid = jnp.where(tx == 1, grid[..., ::-1], grid)
    grid = grid.reshape(docs, 2, 4, 32, 4)
    text_at = grid.transpose(0, 1, 2, 4, 3).reshape(docs, 2, 512)
    own_at = grid[..., 0].reshape(docs, 2, TT)
    place = jnp.arange(512, dtype=jnp.int32)
    relative = (place // 32) % 4
    position = 4 * (place // 128 * 32 + place % 32) + (own_tile ^ relative)
    window = jnp.arange(128, dtype=jnp.int32)
    row0 = ty * (SIDE - HW)
    col0 = tx * (SIDE - HW)
    cell_r = jnp.minimum(window // WIN, WIN - 1) + row0
    cell_c = window % WIN + col0
    inside = window < WIN * WIN
    window_at = jnp.stack([patch_level(cell_c), patch_level(cell_r)])
    key_at = jnp.concatenate(
        [text_at, jnp.broadcast_to(window_at, (docs, 2, 128))], axis=2
    )
    live = jnp.concatenate(
        [
            position[None] < lengths[:, None],
            jnp.broadcast_to(inside, (docs, 128)),
        ],
        axis=1,
    )
    penalty = jnp.where(live, 0.0, NEG).astype(F32)
    slot = jnp.arange(SLOT, dtype=jnp.int32)
    slot_at = jnp.stack(
        [
            patch_level(tx * SIDE + slot % SIDE),
            patch_level(ty * SIDE + jnp.minimum(slot // SIDE, SIDE - 1)),
        ]
    )
    query_at = jnp.concatenate([own_at, jnp.broadcast_to(slot_at, (docs, 2, SLOT))], axis=2)
    level = jnp.arange(LEVELS, dtype=jnp.int32)
    key_hot = (key_at[:, :, None, :] == level[None, None, :, None]).astype(BF)
    key_hot = key_hot.reshape(docs, 2 * LEVELS, KEYS)
    hot_rows = jnp.concatenate(
        [(key_at[:, s, :, None] == level).astype(BF) for s in range(2)], axis=2
    )
    query_hot = jnp.concatenate(
        [(query_at[:, s, :, None] == level).astype(BF) for s in range(2)], axis=2
    )
    flip_hot = jnp.concatenate(
        [(query_at[:, s, :, None] == LEVELS - 1 - level).astype(BF) for s in range(2)], axis=2
    )
    mask_rows = jnp.broadcast_to(penalty[:, :, None], (docs, KEYS, 128))
    tile_r = cell_r // SIDE
    tile_c = cell_c // SIDE
    source = (
        (2 * (tile_r ^ ty) + (tile_c ^ tx)) * SLOT + (cell_r % SIDE) * SIDE + cell_c % SIDE
    )
    pick = (
        (source[:, None] == jnp.arange(4 * SLOT, dtype=jnp.int32)[None]) & inside[:, None]
    ).astype(BF)
    step = jnp.arange(256, dtype=jnp.int32)
    offset = jnp.where(step < 128, -step, 256 - step)
    bucket = jnp.clip(offset, -(BUCKETS // 2), BUCKETS // 2 - 1) + BUCKETS // 2
    spread = (jnp.arange(BUCKETS, dtype=jnp.int32)[:, None] == bucket[None]).astype(F32)
    ramp = jnp.dot(bucket_bias.reshape(2 * H, BUCKETS), spread, precision=HIGHEST)
    ramp = ramp.reshape(2, GROUPS, GH, 256).transpose(1, 0, 2, 3).reshape(GROUPS, 8, 256)

    per_doc = lambda *dims: pl.BlockSpec((1,) + dims, lambda g, d, *_: (d,) + (0,) * len(dims))
    by_group = lambda rows, col: pl.BlockSpec((rows, GW), lambda g, d, *_: (0, col + g))
    doc_group = lambda rows: pl.BlockSpec((1, rows, GW), lambda g, d, *_: (d, 0, g))

    keys, q, k, v, mix, lse, bias = call(
        forward_kernel,
        (GROUPS, docs),
        [
            per_doc(ROWS, D), per_doc(ROWS, D), per_doc(ROWS, D), per_doc(ROWS, D),
            whole((128, 4 * SLOT)),
            by_group(D, 0), by_group(D, GROUPS), by_group(D, 2 * GROUPS),
            by_group(1, 0), by_group(1, 0),
            per_doc(2 * LEVELS, KEYS), per_doc(1, KEYS), per_doc(ROWS, 2 * LEVELS),
            pl.BlockSpec((1, 8, 256), lambda g, d: (g, 0, 0)),
        ],
        [
            pl.BlockSpec((1, KEYS, D), lambda g, d: (jnp.where(g == 0, d, docs - 1), 0, 0)),
            doc_group(ROWS), doc_group(KEYS), doc_group(KEYS), doc_group(ROWS),
            pl.BlockSpec((1, 1, 8, ROWS), lambda g, d: (d, g, 0, 0)),
            pl.BlockSpec((1, GH, ROWS, 256), lambda g, d: (d, g, 0, 0)),
        ],
        [
            shape((docs, KEYS, D), BF), shape((docs, ROWS, D), BF), shape((docs, KEYS, D), BF),
            shape((docs, KEYS, D), BF), shape((docs, ROWS, D), BF),
            shape((docs, GROUPS, 8, ROWS), F32), shape((docs, H, ROWS, 256), BF),
        ],
        [pltpu.VMEM((docs, KEYS, D), BF), pltpu.VMEM((GH, LEVELS, 256), BF)],
        prefetch=0,
        cost=(20_000_000_000, 20_000_000),
    )(
        low_rows, core_rows, side_rows, diag_rows, pick, wp, wp, wp,
        query_bias.reshape(1, D), value_bias.reshape(1, D), key_hot, penalty[:, None, :],
        query_hot, ramp,
    )

    vec = lambda n: whole((1, n))
    flat = lambda: whole((total, D))
    up_at = lambda i, s: jnp.minimum(i, CHUNKS - 1)
    mix2 = mix.reshape(total, D)
    half = CHUNKS // 2
    (
        normed, inv, low, slope, text_res, patch_res, dz, df, vec_feed, down_keep, down_send,
    ) = call(
        feed_kernel,
        (2 * CHUNKS,),
        [
            flat(), whole((docs, TT, D)), whole((docs, SIDE, SIDE, D)), whole((docs, TT, D)),
            whole((docs, SIDE, SIDE, D)), whole((D, D)),
            pl.BlockSpec((D, FC), lambda i, s: (0, up_at(i, s))),
            pl.BlockSpec((FC, D), lambda i, s: (up_at(i, s), 0)),
            vec(D), vec(D), vec(D), pl.BlockSpec((1, FC), lambda i, s: (0, up_at(i, s))),
            vec(D), vec(D), vec(D),
        ],
        [
            flat(), whole((total, 128)), flat(),
            pl.BlockSpec((total, FC), lambda i, s: (0, up_at(i, s))),
            whole((docs, TT, D)), whole((docs, SIDE, SIDE, D)), flat(), flat(), whole((8, D)),
            pl.BlockSpec((D, FC), lambda i, s: (0, jnp.clip(i - CHUNKS, 0, half - 1))),
            pl.BlockSpec((D, FC), lambda i, s: (0, jnp.clip(i - CHUNKS - half, 0, half - 1))),
        ],
        [
            shape((total, D), F32), shape((total, 128), F32), shape((total, D), BF),
            shape((total, FF), F32), shape((docs, TT, D), F32),
            shape((docs, SIDE, SIDE, D), F32), shape((total, D), F32), shape((total, D), BF),
            shape((8, D), F32), shape((D, FF // 2), BF), shape((D, FF // 2), BF),
        ],
        [
            pltpu.VMEM((total, D), F32), pltpu.VMEM((total, D), F32), pltpu.VMEM((total, D), BF),
            pltpu.VMEM((total, D), F32), pltpu.VMEM((CHUNKS, total, FC), BF),
            pltpu.VMEM((total, D), BF),
        ],
        cost=(9_000_000_000, 40_000_000),
    )(
        info, mix2, text, patch_rows, text_cot, patch_cotangent, wo, wu, wd,
        out_bias.reshape(1, D), gain_one.reshape(1, D), shift_one.reshape(1, D),
        up_bias.reshape(1, FF), down_bias.reshape(1, D), gain_two.reshape(1, D),
        shift_two.reshape(1, D),
    )

    bu_grad, vec_back, dh, do, up_keep, up_send, out_keep, out_send = call(
        feed_back_kernel,
        (CHUNKS,),
        [
            flat(), flat(), pl.BlockSpec((total, FC), lambda i, s: (0, i)), flat(), flat(),
            whole((total, 128)), flat(), whole((D, D)),
            pl.BlockSpec((D, FC), lambda i, s: (0, i)),
            pl.BlockSpec((FC, D), lambda i, s: (i, 0)), vec(D),
        ],
        [
            pl.BlockSpec((1, FC), lambda i, s: (0, i)), whole((8, D)), flat(), flat(),
            pl.BlockSpec((FC, HALF), lambda i, s: (i, 0)),
            pl.BlockSpec((FC, HALF), lambda i, s: (i, 0)),
            whole((D, HALF)), whole((D, HALF)),
        ],
        [
            shape((1, FF), F32), shape((8, D), F32), shape((total, D), F32),
            shape((total, D), BF), shape((FF, HALF), BF), shape((FF, HALF), BF),
            shape((D, HALF), BF), shape((D, HALF), BF),
        ],
        [pltpu.VMEM((total, D), F32)],
        cost=(10_000_000_000, 40_000_000),
    )(info, df, dz, slope, low, normed, inv, mix2, wo, wu, wd, gain_one.reshape(1, D))

    dq, dk, dv, wp_keep, wp_send, qb_grad, vb_grad, bucket_grad = call(
        backward_kernel,
        (GROUPS, docs),
        [
            per_doc(KEYS, D), per_doc(ROWS, D), doc_group(ROWS), doc_group(KEYS),
            doc_group(KEYS), doc_group(ROWS), doc_group(ROWS),
            pl.BlockSpec((1, 1, 8, ROWS), lambda g, d, s: (d, g, 0, 0)),
            pl.BlockSpec((1, GH, ROWS, 256), lambda g, d, s: (d, g, 0, 0)),
            per_doc(2 * LEVELS, KEYS), per_doc(KEYS, 2 * LEVELS), per_doc(ROWS, 2 * LEVELS),
            per_doc(KEYS, 128),
        ],
        [
            doc_group(ROWS), doc_group(KEYS), doc_group(KEYS),
            pl.BlockSpec((3, GW, HALF), lambda g, d, s: (0, g, 0)),
            pl.BlockSpec((3, GW, HALF), lambda g, d, s: (0, g, 0)),
            by_group(1, 0), by_group(1, 0),
            pl.BlockSpec((1, 8, BUCKETS), lambda g, d, s: (g, 0, 0)),
        ],
        [
            shape((docs, ROWS, D), BF), shape((docs, KEYS, D), BF), shape((docs, KEYS, D), BF),
            shape((3, D, HALF), BF), shape((3, D, HALF), BF), shape((1, D), F32),
            shape((1, D), F32), shape((GROUPS, 8, BUCKETS), F32),
        ],
        [
            pltpu.VMEM((3 * GW, D), F32), pltpu.VMEM((GH, 2, LEVELS, LEVELS), F32),
            pltpu.VMEM((8, GW), F32),
        ],
        cost=(30_000_000_000, 30_000_000),
    )(
        info, keys, low_rows, q, k, v, mix, do.reshape(docs, ROWS, D), lse, bias, key_hot,
        hot_rows, flip_hot, mask_rows,
    )

    one = lambda *dims: pl.BlockSpec((1,) + dims, lambda d: (d,) + (0,) * len(dims))
    own, cross, side = call(
        input_kernel,
        (docs,),
        [
            one(ROWS, D), one(KEYS, D), one(KEYS, D), one(ROWS, D), whole((128, 4 * SLOT)),
            pl.BlockSpec((D, D), lambda d: (0, 0)), pl.BlockSpec((D, D), lambda d: (0, 1)),
            pl.BlockSpec((D, D), lambda d: (0, 2)),
        ],
        [
            one(ROWS, D), pl.BlockSpec((2, 1, ROWS, D), lambda d: (0, d, 0, 0)), one(ROWS, D),
        ],
        [
            shape((docs, ROWS, D), F32), shape((2, docs, ROWS, D), BF),
            shape((docs, ROWS, D), BF),
        ],
        [pltpu.VMEM((KEYS, D), F32)],
        prefetch=0,
        cost=(5_500_000_000, 20_000_000),
    )(dq, dk, dv, dh.reshape(docs, ROWS, D), pick, wp, wp, wp)
    cross = swap(cross, "tx")
    side = swap(added(side, cross[1]), "ty")
    text_grad, patch_grad = call(
        final_kernel,
        (docs,),
        [one(ROWS, D), pl.BlockSpec((1, 1, ROWS, D), lambda d: (0, d, 0, 0)), one(ROWS, D)],
        [one(TT, D), one(SIDE, SIDE, D)],
        [shape((docs, TT, D), F32), shape((docs, SIDE, SIDE, D), F32)],
        [pltpu.VMEM((ROWS, D), F32)],
        prefetch=0,
        cost=(1_000_000, 10_000_000),
    )(own, cross, side)

    count = lax.axis_size("docs")
    down_sum = gathered(reduced(down_keep, down_send, D // count, True))
    up_sum = gathered(reduced(up_keep, up_send, FF // count, False))
    out_sum = gathered(reduced(out_keep, out_send, D // count, True))
    wp_sum = gathered(
        reduced(
            wp_keep.reshape(3 * D, HALF), wp_send.reshape(3 * D, HALF), 3 * D // count, False
        )
    )

    bucket_grad = bucket_grad.reshape(GROUPS, 2, GH, BUCKETS).transpose(1, 0, 2, 3)
    vectors = [
        qb_grad, vb_grad, vec_back[2], vec_back[0], vec_back[1], bu_grad, vec_feed[2],
        vec_feed[0], vec_feed[1], bucket_grad,
    ]
    sizes = [v.size // count for v in vectors]
    packed = jnp.concatenate([v.reshape(count, -1) for v in vectors], axis=1)
    packed = packed + swap(packed, "tx")
    packed = packed + swap(packed, "ty")
    bits = count.bit_length() - 1
    packed = docs_stages(packed.reshape((2,) * bits + (packed.shape[1],)), 0)
    sums = []
    at = 0
    for size in sizes:
        sums.append(packed[at : at + size])
        at += size
    qb_sum, vb_sum, ob_sum, g1_sum, s1_sum, bu_sum, bd_sum, g2_sum, s2_sum, bucket_sum = sums
    return (
        text_res.reshape(docs, TT, 1, D),
        patch_res,
        text_grad.reshape(docs, TT, 1, D),
        patch_grad,
        wp_sum,
        qb_sum,
        vb_sum,
        out_sum,
        ob_sum,
        g1_sum,
        s1_sum,
        up_sum,
        bu_sum,
        down_sum,
        bd_sum,
        g2_sum,
        s2_sum,
        bucket_sum,
    )


def solution(mesh):
    in_specs = (
        P("docs", None, ("ty", "tx"), None),
        P("docs", "ty", "tx", None),
        P("docs", None, None),
        P("docs"),
    ) + (P(),) * 14 + (
        P("docs", None, ("ty", "tx"), None),
        P("docs", "ty", "tx", None),
    )
    out_specs = (
        P("docs", None, ("ty", "tx"), None),
        P("docs", "ty", "tx", None),
        P("docs", None, ("ty", "tx"), None),
        P("docs", "ty", "tx", None),
        P(None, "docs"),
        P("docs"),
        P("docs"),
        P(None, "docs"),
        P("docs"),
        P("docs"),
        P("docs"),
        P(None, "docs"),
        P("docs"),
        P(None, "docs"),
        P("docs"),
        P("docs"),
        P("docs"),
        P("docs"),
    )
    return jax.shard_map(shards, mesh=mesh, in_specs=in_specs, out_specs=out_specs, check_vma=False)
```

```python
import functools

import jax
import jax.numpy as jnp
from jax import lax
from jax.experimental import pallas as pl
from jax.experimental.pallas import tpu as pltpu
from jax.sharding import PartitionSpec as P

D = 768
H = 12
DH = 64
FF = 3072
BUCKETS = 64
LEVELS = 128
GRID = 14
HW = 3
TT = 128

EPSILON = 1e-05
HIGHEST = lax.Precision.HIGHEST
SIDE = 7
CELLS = SIDE * SIDE
ROWS = 192
SLOT = ROWS - TT
WIN = SIDE + HW
KEYS = 640
GROUPS = 3
GH = H // GROUPS
GW = GH * DH
CHUNKS = 6
FC = FF // CHUNKS
HALF = D // 2
BF = jnp.bfloat16
F32 = jnp.float32
NEG = -1e30


def dot(a, b, ca=1, cb=0, precision=None):
    return lax.dot_general(
        a, b, (((ca,), (cb,)), ((), ())), preferred_element_type=F32, precision=precision
    )


def call(kernel, grid, ins, outs, shapes, scratch=(), prefetch=1, cost=(0, 0)):
    return pl.pallas_call(
        kernel,
        grid_spec=pltpu.PrefetchScalarGridSpec(
            num_scalar_prefetch=prefetch,
            grid=grid,
            in_specs=ins,
            out_specs=outs,
            scratch_shapes=list(scratch),
        ),
        out_shape=shapes,
        compiler_params=pltpu.CompilerParams(
            dimension_semantics=("arbitrary",) * len(grid), vmem_limit_bytes=60 << 20
        ),
        cost_estimate=pl.CostEstimate(flops=cost[0], bytes_accessed=cost[1], transcendentals=0),
    )


def whole(shape):
    return pl.BlockSpec(shape, lambda *_: (0,) * len(shape))


def shape(dims, dtype):
    return jax.ShapeDtypeStruct(dims, dtype)


def put_rows(dst, base, text, patch, cast):
    dst[base : base + TT] = cast(text)
    for i in range(SIDE):
        dst[base + TT + SIDE * i : base + TT + SIDE * (i + 1)] = cast(patch[i])
    dst[base + TT + CELLS : base + ROWS] = jnp.zeros((SLOT - CELLS, D), dst.dtype)


def rows_kernel(text, patch, low, buf):
    put_rows(buf, 0, text[0], patch[0], lambda v: v)
    low[0] = buf[...].astype(BF)


def forward_kernel(
    own, core, side, diag, pick, wq, wk, wv, qb, vb, key_hot, mask, query_hot, ramp,
    keys_out, q_out, k_out, v_out, mix_out, lse_out, bias_out, keys, table,
):
    g = pl.program_id(0)
    d = pl.program_id(1)

    @pl.when(g == 0)
    def _():
        tiles = (own, core, side, diag)
        for c in range(4):
            for r in range(4):
                at = c * 128 + r * 32
                keys[d, at : at + 32] = tiles[r][0, c * 32 : c * 32 + 32]
        cells = jnp.concatenate([t[0, TT:] for t in tiles], axis=0)
        keys[d, 512:KEYS] = dot(pick[...], cells).astype(BF)

    @pl.when(g == 0)
    def _():
        keys_out[0] = keys[d]

    @pl.when(d == 0)
    def _():
        for h in range(GH):
            for s in range(2):
                line = jnp.broadcast_to(ramp[0, s * GH + h : s * GH + h + 1], (LEVELS, 256))
                rolled = pltpu.roll(line, 0, 1, stride=1, stride_axis=0)
                table[h, :, s * LEVELS : (s + 1) * LEVELS] = rolled[:, :LEVELS].astype(BF)

    rows = keys[d]
    key4 = dot(rows, wk[...].astype(BF)).astype(BF)
    value4 = (dot(rows, wv[...].astype(BF)) + vb[...]).astype(BF)
    query4 = ((dot(own[0], wq[...].astype(BF)) + qb[...]) * 0.125).astype(BF)
    k_out[0] = key4
    v_out[0] = value4
    q_out[0] = query4
    lane = lax.broadcasted_iota(jnp.int32, (ROWS, 128), 1)
    hot = query_hot[0]
    logs = jnp.zeros((ROWS, 128), F32)
    for p in range(2):
        cut = slice(128 * p, 128 * (p + 1))
        pieces = []
        for half in range(2):
            h = 2 * p + half
            mine = (lane < DH) if half == 0 else (lane >= DH)
            masked = jnp.where(mine, query4[:, cut], jnp.zeros((), BF))
            tab = table[h]
            shift = jnp.concatenate(
                [
                    dot(hot[:, :LEVELS], tab[:, :LEVELS]).astype(BF),
                    dot(hot[:, LEVELS:], tab[:, LEVELS:]).astype(BF),
                ],
                axis=1,
            )
            bias_out[0, h] = shift
            score = dot(masked, key4[:, cut], 1, 1) + dot(shift, key_hot[0]) + mask[0]
            top = jnp.max(score, axis=1, keepdims=True)
            power = jnp.exp(score - top)
            total = jnp.sum(power, axis=1, keepdims=True)
            mixed = dot(power.astype(BF), value4[:, cut]) / total
            pieces.append(mixed)
            logs = jnp.where(lane == h, top + jnp.log(total), logs)
        mix_out[0, :, cut] = jnp.where(lane < DH, pieces[0], pieces[1]).astype(BF)
    lse_out[0, 0] = jnp.transpose(logs)[:8]


def stats(v):
    center = v - jnp.mean(v, axis=-1, keepdims=True)
    inv = lax.rsqrt(jnp.mean(center * center, axis=-1, keepdims=True) + EPSILON)
    return center * inv, inv


def back_norm(grad, normed, inv):
    return inv * (
        grad
        - jnp.mean(grad, axis=-1, keepdims=True)
        - normed * jnp.mean(grad * normed, axis=-1, keepdims=True)
    )


def feed_kernel(
    info, mix, text, patch, text_cot, patch_cot, wo, wu, wd, bo, g1, s1, bu, bd, g2, s2,
    norm_out, inv_out, low_out, slope_out, text_out, patch_out, dz_out, df_out, vec_out,
    keep_out, send_out, buf, hidden, low, feed, active, df,
):
    i = pl.program_id(0)
    docs = text.shape[0]
    total = docs * ROWS

    @pl.when(i == 0)
    def _():
        for d in range(docs):
            put_rows(buf, d * ROWS, text[d], patch[d], lambda v: v)
        normed, inv = stats(buf[...] + (dot(mix[...], wo[...].astype(BF)) + bo[...]))
        norm_out[...] = normed
        inv_out[...] = jnp.broadcast_to(inv, (total, 128))
        out = normed * g1[...] + s1[...]
        hidden[...] = out
        low[...] = out.astype(BF)
        low_out[...] = out.astype(BF)
        feed[...] = jnp.zeros_like(feed)

    @pl.when(i < CHUNKS)
    def _():
        u = dot(low[...], wu[...].astype(BF)) + bu[...]
        phi = 0.5 * (1.0 + lax.erf(u * 0.7071067811865476))
        slope_out[...] = phi + u * (0.3989422804014327 * jnp.exp(-0.5 * u * u))
        act = (u * phi).astype(BF)
        active[i] = act
        feed[...] += dot(act, wd[...].astype(BF))

    @pl.when(i == CHUNKS - 1)
    def _():
        normed, inv = stats(hidden[...] + (feed[...] + bd[...]))
        row = lax.broadcasted_iota(jnp.int32, (total, 1), 0)
        live = jnp.zeros((total, 1), F32)
        for d in range(docs):
            at = row - d * ROWS
            ok = (at >= 0) & (at < ROWS) & ((at >= TT) | (4 * at + info[1] < info[2 + d]))
            live = jnp.where(ok, 1.0, live)
        feed[...] = (normed * g2[...] + s2[...]) * live
        for d in range(docs):
            base = d * ROWS
            text_out[d] = feed[base : base + TT]
            for k in range(SIDE):
                at = base + TT + SIDE * k
                patch_out[d, k] = feed[at : at + SIDE]
        for d in range(docs):
            put_rows(buf, d * ROWS, text_cot[d], patch_cot[d], lambda v: v)
        cot = buf[...] * live
        vec_out[0:1] = jnp.sum(cot * normed, axis=0, keepdims=True)
        vec_out[1:2] = jnp.sum(cot, axis=0, keepdims=True)
        dz = back_norm(cot * g2[...], normed, inv)
        dz_out[...] = dz
        df[...] = dz.astype(BF)
        df_out[...] = dz.astype(BF)
        vec_out[2:3] = jnp.sum(dz.astype(BF).astype(F32), axis=0, keepdims=True)
        vec_out[3:8] = jnp.zeros((5, D), F32)

    k = i - CHUNKS
    half = CHUNKS // 2

    @pl.when((i >= CHUNKS) & (k < half))
    def _():
        keep_out[...] = dot(df[...], active[half * info[0] + k], 0, 0).astype(BF)

    @pl.when((i >= CHUNKS) & (k >= half))
    def _():
        send_out[...] = dot(df[...], active[half * (1 - info[0]) + k - half], 0, 0).astype(BF)


def feed_back_kernel(
    info, df, dz, slope, low, normed, inv, mix, wo, wu, wd, g1,
    bu_out, vec_out, dh_out, do_out, up_keep, up_send, out_keep, out_send, acc,
):
    i = pl.program_id(0)
    first = info[0] == 0

    @pl.when(i == 0)
    def _():
        acc[...] = dz[...]

    du32 = dot(df[...], wd[...].astype(BF), 1, 1) * slope[...]
    du = du32.astype(BF)
    bu_out[...] = jnp.sum(du.astype(F32), axis=0, keepdims=True)
    acc[...] += dot(du, wu[...].astype(BF), 1, 1)
    grad = dot(du, low[...], 0, 0)
    up_keep[...] = jnp.where(first, grad[:, :HALF], grad[:, HALF:]).astype(BF)
    up_send[...] = jnp.where(first, grad[:, HALF:], grad[:, :HALF]).astype(BF)

    @pl.when(i == CHUNKS - 1)
    def _():
        dy = acc[...]
        n1 = normed[...]
        vec_out[0:1] = jnp.sum(dy * n1, axis=0, keepdims=True)
        vec_out[1:2] = jnp.sum(dy, axis=0, keepdims=True)
        dh = back_norm(dy * g1[...], n1, inv[:, 0:1])
        dh_out[...] = dh
        da = dh.astype(BF)
        vec_out[2:3] = jnp.sum(da.astype(F32), axis=0, keepdims=True)
        vec_out[3:8] = jnp.zeros((5, D), F32)
        do_out[...] = dot(da, wo[...].astype(BF), 1, 1).astype(BF)
        grad = dot(da, mix[...], 0, 0)
        out_keep[...] = jnp.where(first, grad[:, :HALF], grad[:, HALF:]).astype(BF)
        out_send[...] = jnp.where(first, grad[:, HALF:], grad[:, :HALF]).astype(BF)


def backward_kernel(
    info, keys, own, q, k, v, mix, do, lse, bias, key_hot, hot_rows, flip_hot, mask,
    dq_out, dk_out, dv_out, keep_out, send_out, qb_out, vb_out, bucket_out, acc, maps, sums,
):
    d = pl.program_id(1)
    last = pl.num_programs(1) - 1
    first = info[0] == 0

    @pl.when(d == 0)
    def _():
        acc[...] = jnp.zeros_like(acc)
        maps[...] = jnp.zeros_like(maps)
        sums[...] = jnp.zeros_like(sums)

    lane = lax.broadcasted_iota(jnp.int32, (ROWS, 128), 1)
    head = lax.broadcasted_iota(jnp.int32, (8, GW), 0)
    span = lax.broadcasted_iota(jnp.int32, (8, GW), 1) // DH
    pick = (head == span).astype(F32)
    do4 = do[0]
    q4 = q[0]
    delta = dot(pick, do4.astype(F32) * mix[0].astype(F32), 1, 1, HIGHEST)
    zero = jnp.zeros((), BF)
    for p in range(2):
        cut = slice(128 * p, 128 * (p + 1))
        kp = k[0, :, cut]
        vp = v[0, :, cut]
        kt = jnp.transpose(kp)
        dk = jnp.zeros((KEYS, 128), F32)
        dv = jnp.zeros((KEYS, 128), F32)
        dq = []
        for half in range(2):
            h = 2 * p + half
            mine = (lane < DH) if half == 0 else (lane >= DH)
            qm = jnp.where(mine, q4[:, cut], zero)
            dm = jnp.where(mine, do4[:, cut], zero)
            score = dot(kp, qm, 1, 1) + dot(hot_rows[0], bias[0, h], 1, 1)
            prob = jnp.exp(score + (jnp.concatenate([mask[0], mask[0, :, :64]], axis=1) - lse[0, 0, h : h + 1]))
            grad = dot(vp, dm, 1, 1) - delta[h : h + 1]
            ds = (prob * grad).astype(BF)
            dv = dv + dot(prob.astype(BF), dm)
            dk = dk + dot(ds, qm)
            dq.append(dot(kt[DH * half : DH * (half + 1)], ds))
            by_key = dot(key_hot[0], ds).astype(BF)
            for s in range(2):
                maps[h, s] += dot(by_key[LEVELS * s : LEVELS * (s + 1)], flip_hot[0, :, LEVELS * s : LEVELS * (s + 1)])
        dk_out[0, :, cut] = dk.astype(BF)
        dv_out[0, :, cut] = dv.astype(BF)
        dq_out[0, :, cut] = jnp.transpose(jnp.concatenate(dq, axis=0)).astype(BF) * 0.125
    dq4 = dq_out[0]
    dk4 = dk_out[0]
    dv4 = dv_out[0]
    acc[0:GW] += dot(dq4, own[0], 0, 0)
    acc[GW : 2 * GW] += dot(dk4, keys[0], 0, 0)
    acc[2 * GW :] += dot(dv4, keys[0], 0, 0)
    sums[0:1] += jnp.sum(dq4.astype(F32), axis=0, keepdims=True)
    sums[1:2] += jnp.sum(dv4.astype(F32), axis=0, keepdims=True)

    @pl.when(d == last)
    def _():
        for s in range(3):
            grad = acc[s * GW : (s + 1) * GW]
            keep_out[s] = jnp.where(first, grad[:, :HALF], grad[:, HALF:]).astype(BF)
            send_out[s] = jnp.where(first, grad[:, HALF:], grad[:, :HALF]).astype(BF)
        qb_out[...] = sums[0:1]
        vb_out[...] = sums[1:2]
        at = lax.broadcasted_iota(jnp.int32, (256, BUCKETS), 0)
        bucket = jnp.clip(LEVELS - 1 - at, -(BUCKETS // 2), BUCKETS // 2 - 1) + BUCKETS // 2
        to_bucket = (bucket == lax.broadcasted_iota(jnp.int32, (256, BUCKETS), 1)).astype(F32)
        lines = []
        for s in range(2):
            for h in range(GH):
                wide = jnp.concatenate([maps[h, s], jnp.zeros((LEVELS, LEVELS), F32)], axis=1)
                lines.append(jnp.sum(pltpu.roll(wide, 0, 1, stride=1, stride_axis=0), axis=0, keepdims=True))
        bucket_out[0] = dot(jnp.concatenate(lines, axis=0), to_bucket, 1, 0, HIGHEST)


def input_kernel(dq, dk, dv, dh, pick, wq, wk, wv, own_out, cross_out, side_out, part):
    part[...] = dot(dk[0], wk[...].astype(BF), 1, 1) + dot(
        dv[0], wv[...].astype(BF), 1, 1
    )
    query = dot(dq[0], wq[...].astype(BF), 1, 1)
    cells = dot(pick[...], part[512:KEYS].astype(BF), 0, 0)

    def emit(r, store):
        for c in range(4):
            at = c * 128 + r * 32
            store(slice(c * 32, c * 32 + 32), part[at : at + 32])
        store(slice(TT, ROWS), cells[r * SLOT : (r + 1) * SLOT])

    def own_store(at, value):
        own_out[0, at] = dh[0, at] + (query[at] + value)

    def core_store(at, value):
        cross_out[0, 0, at] = value.astype(BF)

    def diag_store(at, value):
        cross_out[1, 0, at] = value.astype(BF)

    def side_store(at, value):
        side_out[0, at] = value.astype(BF)

    emit(0, own_store)
    emit(1, core_store)
    emit(2, side_store)
    emit(3, diag_store)


def final_kernel(own, cross, side, text_out, patch_out, buf):
    buf[...] = own[0] + cross[0, 0].astype(F32) + side[0].astype(F32)
    text_out[0] = buf[:TT]
    for i in range(SIDE):
        at = TT + SIDE * i
        patch_out[0, i] = buf[at : at + SIDE]


def patch_level(cell_index):
    return (2 * cell_index + 1) * LEVELS // (2 * GRID)


def swap(value, axis):
    return lax.ppermute(value, axis, [(0, 1), (1, 0)])


def exchange(value, axis, mask):
    count = lax.axis_size(axis)
    return lax.ppermute(value, axis, [(i, i ^ mask) for i in range(count)])


def added(a, b):
    return (a.astype(F32) + b.astype(F32)).astype(a.dtype)


def halves(value, bit, dim):
    keep = lax.dynamic_index_in_dim(value, bit, dim, keepdims=False)
    send = lax.dynamic_index_in_dim(value, 1 - bit, dim, keepdims=False)
    return keep, send


def docs_stages(value, lead):
    count = lax.axis_size("docs")
    bits = count.bit_length() - 1
    here = lax.axis_index("docs")
    for b in range(bits):
        dim = lead + bits - 1 - b
        keep, send = halves(value, (here >> b) & 1, dim)
        value = added(keep, exchange(send, "docs", 1 << b))
    return value


def tile_half(value, axis, bit):
    keep, send = halves(value, bit, axis)
    return added(keep, swap(send, "ty"))


def reduced(keep, send, rows, side_first):
    count = lax.axis_size("docs")
    bits = count.bit_length() - 1
    ty = lax.axis_index("ty")
    columns = keep.shape[-1]
    value = added(keep, swap(send, "tx"))
    value = value.reshape((2,) * bits + (2, rows // 2, columns))
    if side_first:
        value = tile_half(value, bits, ty)
        value = docs_stages(value, 0)
    else:
        value = docs_stages(value, 0)
        value = tile_half(value, 0, ty)
    return value


def joined(value, axis, dim):
    other = swap(value, axis)
    low = lax.axis_index(axis) == 0
    return jnp.concatenate(
        [jnp.where(low, value, other), jnp.where(low, other, value)], axis=dim
    )


def gathered(value):
    return joined(joined(value, "ty", 0), "tx", 1).astype(F32).T


def shards(
    text_rows,
    patch_rows,
    text_boxes,
    lengths,
    project_weight,
    query_bias,
    value_bias,
    out_weight,
    out_bias,
    gain_one,
    shift_one,
    up_weight,
    up_bias,
    down_weight,
    down_bias,
    gain_two,
    shift_two,
    bucket_bias,
    text_cotangent,
    patch_cotangent,
):
    docs = text_rows.shape[0]
    total = docs * ROWS
    tx = lax.axis_index("tx")
    ty = lax.axis_index("ty")
    own_tile = 2 * ty + tx
    info = jnp.concatenate([jnp.stack([tx, own_tile]).astype(jnp.int32), lengths])
    text = text_rows.reshape(docs, TT, D)
    text_cot = text_cotangent.reshape(docs, TT, D)

    low_rows = pl.pallas_call(
        rows_kernel,
        grid=(docs,),
        in_specs=[
            pl.BlockSpec((1, TT, D), lambda d: (d, 0, 0)),
            pl.BlockSpec((1, SIDE, SIDE, D), lambda d: (d, 0, 0, 0)),
        ],
        out_specs=pl.BlockSpec((1, ROWS, D), lambda d: (d, 0, 0)),
        out_shape=shape((docs, ROWS, D), BF),
        scratch_shapes=[pltpu.VMEM((ROWS, D), F32)],
    )(text, patch_rows)
    side_rows = swap(low_rows, "ty")
    core_rows = swap(low_rows, "tx")
    diag_rows = swap(side_rows, "tx")

    wp = project_weight
    wo = out_weight
    wu = up_weight
    wd = down_weight

    grid = text_boxes.reshape(docs, 2, TT, 2, 2)
    grid = jnp.where(ty == 1, grid[:, :, :, ::-1], grid)
    grid = jnp.where(tx == 1, grid[..., ::-1], grid)
    grid = grid.reshape(docs, 2, 4, 32, 4)
    text_at = grid.transpose(0, 1, 2, 4, 3).reshape(docs, 2, 512)
    own_at = grid[..., 0].reshape(docs, 2, TT)
    place = jnp.arange(512, dtype=jnp.int32)
    relative = (place // 32) % 4
    position = 4 * (place // 128 * 32 + place % 32) + (own_tile ^ relative)
    window = jnp.arange(128, dtype=jnp.int32)
    row0 = ty * (SIDE - HW)
    col0 = tx * (SIDE - HW)
    cell_r = jnp.minimum(window // WIN, WIN - 1) + row0
    cell_c = window % WIN + col0
    inside = window < WIN * WIN
    window_at = jnp.stack([patch_level(cell_c), patch_level(cell_r)])
    key_at = jnp.concatenate(
        [text_at, jnp.broadcast_to(window_at, (docs, 2, 128))], axis=2
    )
    live = jnp.concatenate(
        [
            position[None] < lengths[:, None],
            jnp.broadcast_to(inside, (docs, 128)),
        ],
        axis=1,
    )
    penalty = jnp.where(live, 0.0, NEG).astype(F32)
    slot = jnp.arange(SLOT, dtype=jnp.int32)
    slot_at = jnp.stack(
        [
            patch_level(tx * SIDE + slot % SIDE),
            patch_level(ty * SIDE + jnp.minimum(slot // SIDE, SIDE - 1)),
        ]
    )
    query_at = jnp.concatenate([own_at, jnp.broadcast_to(slot_at, (docs, 2, SLOT))], axis=2)
    level = jnp.arange(LEVELS, dtype=jnp.int32)
    key_hot = (key_at[:, :, None, :] == level[None, None, :, None]).astype(BF)
    key_hot = key_hot.reshape(docs, 2 * LEVELS, KEYS)
    hot_rows = jnp.concatenate(
        [(key_at[:, s, :, None] == level).astype(BF) for s in range(2)], axis=2
    )
    query_hot = jnp.concatenate(
        [(query_at[:, s, :, None] == level).astype(BF) for s in range(2)], axis=2
    )
    flip_hot = jnp.concatenate(
        [(query_at[:, s, :, None] == LEVELS - 1 - level).astype(BF) for s in range(2)], axis=2
    )
    mask_rows = jnp.broadcast_to(penalty[:, :, None], (docs, KEYS, 128))
    tile_r = cell_r // SIDE
    tile_c = cell_c // SIDE
    source = (
        (2 * (tile_r ^ ty) + (tile_c ^ tx)) * SLOT + (cell_r % SIDE) * SIDE + cell_c % SIDE
    )
    pick = (
        (source[:, None] == jnp.arange(4 * SLOT, dtype=jnp.int32)[None]) & inside[:, None]
    ).astype(BF)
    step = jnp.arange(256, dtype=jnp.int32)
    offset = jnp.where(step < 128, -step, 256 - step)
    bucket = jnp.clip(offset, -(BUCKETS // 2), BUCKETS // 2 - 1) + BUCKETS // 2
    spread = (jnp.arange(BUCKETS, dtype=jnp.int32)[:, None] == bucket[None]).astype(F32)
    ramp = jnp.dot(bucket_bias.reshape(2 * H, BUCKETS), spread, precision=HIGHEST)
    ramp = ramp.reshape(2, GROUPS, GH, 256).transpose(1, 0, 2, 3).reshape(GROUPS, 8, 256)

    per_doc = lambda *dims: pl.BlockSpec((1,) + dims, lambda g, d, *_: (d,) + (0,) * len(dims))
    by_group = lambda rows, col: pl.BlockSpec((rows, GW), lambda g, d, *_: (0, col + g))
    doc_group = lambda rows: pl.BlockSpec((1, rows, GW), lambda g, d, *_: (d, 0, g))

    keys, q, k, v, mix, lse, bias = call(
        forward_kernel,
        (GROUPS, docs),
        [
            per_doc(ROWS, D), per_doc(ROWS, D), per_doc(ROWS, D), per_doc(ROWS, D),
            whole((128, 4 * SLOT)),
            by_group(D, 0), by_group(D, GROUPS), by_group(D, 2 * GROUPS),
            by_group(1, 0), by_group(1, 0),
            per_doc(2 * LEVELS, KEYS), per_doc(1, KEYS), per_doc(ROWS, 2 * LEVELS),
            pl.BlockSpec((1, 8, 256), lambda g, d: (g, 0, 0)),
        ],
        [
            pl.BlockSpec((1, KEYS, D), lambda g, d: (jnp.where(g == 0, d, docs - 1), 0, 0)),
            doc_group(ROWS), doc_group(KEYS), doc_group(KEYS), doc_group(ROWS),
            pl.BlockSpec((1, 1, 8, ROWS), lambda g, d: (d, g, 0, 0)),
            pl.BlockSpec((1, GH, ROWS, 256), lambda g, d: (d, g, 0, 0)),
        ],
        [
            shape((docs, KEYS, D), BF), shape((docs, ROWS, D), BF), shape((docs, KEYS, D), BF),
            shape((docs, KEYS, D), BF), shape((docs, ROWS, D), BF),
            shape((docs, GROUPS, 8, ROWS), F32), shape((docs, H, ROWS, 256), BF),
        ],
        [pltpu.VMEM((docs, KEYS, D), BF), pltpu.VMEM((GH, LEVELS, 256), BF)],
        prefetch=0,
        cost=(20_000_000_000, 20_000_000),
    )(
        low_rows, core_rows, side_rows, diag_rows, pick, wp, wp, wp,
        query_bias.reshape(1, D), value_bias.reshape(1, D), key_hot, penalty[:, None, :],
        query_hot, ramp,
    )

    vec = lambda n: whole((1, n))
    flat = lambda: whole((total, D))
    up_at = lambda i, s: jnp.minimum(i, CHUNKS - 1)
    mix2 = mix.reshape(total, D)
    half = CHUNKS // 2
    (
        normed, inv, low, slope, text_res, patch_res, dz, df, vec_feed, down_keep, down_send,
    ) = call(
        feed_kernel,
        (2 * CHUNKS,),
        [
            flat(), whole((docs, TT, D)), whole((docs, SIDE, SIDE, D)), whole((docs, TT, D)),
            whole((docs, SIDE, SIDE, D)), whole((D, D)),
            pl.BlockSpec((D, FC), lambda i, s: (0, up_at(i, s))),
            pl.BlockSpec((FC, D), lambda i, s: (up_at(i, s), 0)),
            vec(D), vec(D), vec(D), pl.BlockSpec((1, FC), lambda i, s: (0, up_at(i, s))),
            vec(D), vec(D), vec(D),
        ],
        [
            flat(), whole((total, 128)), flat(),
            pl.BlockSpec((total, FC), lambda i, s: (0, up_at(i, s))),
            whole((docs, TT, D)), whole((docs, SIDE, SIDE, D)), flat(), flat(), whole((8, D)),
            pl.BlockSpec((D, FC), lambda i, s: (0, jnp.clip(i - CHUNKS, 0, half - 1))),
            pl.BlockSpec((D, FC), lambda i, s: (0, jnp.clip(i - CHUNKS - half, 0, half - 1))),
        ],
        [
            shape((total, D), F32), shape((total, 128), F32), shape((total, D), BF),
            shape((total, FF), F32), shape((docs, TT, D), F32),
            shape((docs, SIDE, SIDE, D), F32), shape((total, D), F32), shape((total, D), BF),
            shape((8, D), F32), shape((D, FF // 2), BF), shape((D, FF // 2), BF),
        ],
        [
            pltpu.VMEM((total, D), F32), pltpu.VMEM((total, D), F32), pltpu.VMEM((total, D), BF),
            pltpu.VMEM((total, D), F32), pltpu.VMEM((CHUNKS, total, FC), BF),
            pltpu.VMEM((total, D), BF),
        ],
        cost=(9_000_000_000, 40_000_000),
    )(
        info, mix2, text, patch_rows, text_cot, patch_cotangent, wo, wu, wd,
        out_bias.reshape(1, D), gain_one.reshape(1, D), shift_one.reshape(1, D),
        up_bias.reshape(1, FF), down_bias.reshape(1, D), gain_two.reshape(1, D),
        shift_two.reshape(1, D),
    )

    bu_grad, vec_back, dh, do, up_keep, up_send, out_keep, out_send = call(
        feed_back_kernel,
        (CHUNKS,),
        [
            flat(), flat(), pl.BlockSpec((total, FC), lambda i, s: (0, i)), flat(), flat(),
            whole((total, 128)), flat(), whole((D, D)),
            pl.BlockSpec((D, FC), lambda i, s: (0, i)),
            pl.BlockSpec((FC, D), lambda i, s: (i, 0)), vec(D),
        ],
        [
            pl.BlockSpec((1, FC), lambda i, s: (0, i)), whole((8, D)), flat(), flat(),
            pl.BlockSpec((FC, HALF), lambda i, s: (i, 0)),
            pl.BlockSpec((FC, HALF), lambda i, s: (i, 0)),
            whole((D, HALF)), whole((D, HALF)),
        ],
        [
            shape((1, FF), F32), shape((8, D), F32), shape((total, D), F32),
            shape((total, D), BF), shape((FF, HALF), BF), shape((FF, HALF), BF),
            shape((D, HALF), BF), shape((D, HALF), BF),
        ],
        [pltpu.VMEM((total, D), F32)],
        cost=(10_000_000_000, 40_000_000),
    )(info, df, dz, slope, low, normed, inv, mix2, wo, wu, wd, gain_one.reshape(1, D))

    dq, dk, dv, wp_keep, wp_send, qb_grad, vb_grad, bucket_grad = call(
        backward_kernel,
        (GROUPS, docs),
        [
            per_doc(KEYS, D), per_doc(ROWS, D), doc_group(ROWS), doc_group(KEYS),
            doc_group(KEYS), doc_group(ROWS), doc_group(ROWS),
            pl.BlockSpec((1, 1, 8, ROWS), lambda g, d, s: (d, g, 0, 0)),
            pl.BlockSpec((1, GH, ROWS, 256), lambda g, d, s: (d, g, 0, 0)),
            per_doc(2 * LEVELS, KEYS), per_doc(KEYS, 2 * LEVELS), per_doc(ROWS, 2 * LEVELS),
            per_doc(KEYS, 128),
        ],
        [
            doc_group(ROWS), doc_group(KEYS), doc_group(KEYS),
            pl.BlockSpec((3, GW, HALF), lambda g, d, s: (0, g, 0)),
            pl.BlockSpec((3, GW, HALF), lambda g, d, s: (0, g, 0)),
            by_group(1, 0), by_group(1, 0),
            pl.BlockSpec((1, 8, BUCKETS), lambda g, d, s: (g, 0, 0)),
        ],
        [
            shape((docs, ROWS, D), BF), shape((docs, KEYS, D), BF), shape((docs, KEYS, D), BF),
            shape((3, D, HALF), BF), shape((3, D, HALF), BF), shape((1, D), F32),
            shape((1, D), F32), shape((GROUPS, 8, BUCKETS), F32),
        ],
        [
            pltpu.VMEM((3 * GW, D), F32), pltpu.VMEM((GH, 2, LEVELS, LEVELS), F32),
            pltpu.VMEM((8, GW), F32),
        ],
        cost=(30_000_000_000, 30_000_000),
    )(
        info, keys, low_rows, q, k, v, mix, do.reshape(docs, ROWS, D), lse, bias, key_hot,
        hot_rows, flip_hot, mask_rows,
    )

    one = lambda *dims: pl.BlockSpec((1,) + dims, lambda d: (d,) + (0,) * len(dims))
    own, cross, side = call(
        input_kernel,
        (docs,),
        [
            one(ROWS, D), one(KEYS, D), one(KEYS, D), one(ROWS, D), whole((128, 4 * SLOT)),
            pl.BlockSpec((D, D), lambda d: (0, 0)), pl.BlockSpec((D, D), lambda d: (0, 1)),
            pl.BlockSpec((D, D), lambda d: (0, 2)),
        ],
        [
            one(ROWS, D), pl.BlockSpec((2, 1, ROWS, D), lambda d: (0, d, 0, 0)), one(ROWS, D),
        ],
        [
            shape((docs, ROWS, D), F32), shape((2, docs, ROWS, D), BF),
            shape((docs, ROWS, D), BF),
        ],
        [pltpu.VMEM((KEYS, D), F32)],
        prefetch=0,
        cost=(5_500_000_000, 20_000_000),
    )(dq, dk, dv, dh.reshape(docs, ROWS, D), pick, wp, wp, wp)
    cross = swap(cross, "tx")
    side = swap(added(side, cross[1]), "ty")
    text_grad, patch_grad = call(
        final_kernel,
        (docs,),
        [one(ROWS, D), pl.BlockSpec((1, 1, ROWS, D), lambda d: (0, d, 0, 0)), one(ROWS, D)],
        [one(TT, D), one(SIDE, SIDE, D)],
        [shape((docs, TT, D), F32), shape((docs, SIDE, SIDE, D), F32)],
        [pltpu.VMEM((ROWS, D), F32)],
        prefetch=0,
        cost=(1_000_000, 10_000_000),
    )(own, cross, side)

    count = lax.axis_size("docs")
    down_sum = gathered(reduced(down_keep, down_send, D // count, True))
    up_sum = gathered(reduced(up_keep, up_send, FF // count, False))
    out_sum = gathered(reduced(out_keep, out_send, D // count, True))
    wp_sum = gathered(
        reduced(
            wp_keep.reshape(3 * D, HALF), wp_send.reshape(3 * D, HALF), 3 * D // count, False
        )
    )

    bucket_grad = bucket_grad.reshape(GROUPS, 2, GH, BUCKETS).transpose(1, 0, 2, 3)
    vectors = [
        qb_grad, vb_grad, vec_back[2], vec_back[0], vec_back[1], bu_grad, vec_feed[2],
        vec_feed[0], vec_feed[1], bucket_grad,
    ]
    sizes = [v.size // count for v in vectors]
    packed = jnp.concatenate([v.reshape(count, -1) for v in vectors], axis=1)
    packed = packed + swap(packed, "tx")
    packed = packed + swap(packed, "ty")
    bits = count.bit_length() - 1
    packed = docs_stages(packed.reshape((2,) * bits + (packed.shape[1],)), 0)
    sums = []
    at = 0
    for size in sizes:
        sums.append(packed[at : at + size])
        at += size
    qb_sum, vb_sum, ob_sum, g1_sum, s1_sum, bu_sum, bd_sum, g2_sum, s2_sum, bucket_sum = sums
    return (
        text_res.reshape(docs, TT, 1, D),
        patch_res,
        text_grad.reshape(docs, TT, 1, D),
        patch_grad,
        wp_sum,
        qb_sum,
        vb_sum,
        out_sum,
        ob_sum,
        g1_sum,
        s1_sum,
        up_sum,
        bu_sum,
        down_sum,
        bd_sum,
        g2_sum,
        s2_sum,
        bucket_sum,
    )


def solution(mesh):
    in_specs = (
        P("docs", None, ("ty", "tx"), None),
        P("docs", "ty", "tx", None),
        P("docs", None, None),
        P("docs"),
    ) + (P(),) * 14 + (
        P("docs", None, ("ty", "tx"), None),
        P("docs", "ty", "tx", None),
    )
    out_specs = (
        P("docs", None, ("ty", "tx"), None),
        P("docs", "ty", "tx", None),
        P("docs", None, ("ty", "tx"), None),
        P("docs", "ty", "tx", None),
        P(None, "docs"),
        P("docs"),
        P("docs"),
        P(None, "docs"),
        P("docs"),
        P("docs"),
        P("docs"),
        P(None, "docs"),
        P("docs"),
        P(None, "docs"),
        P("docs"),
        P("docs"),
        P("docs"),
        P("docs"),
    )
    return jax.shard_map(shards, mesh=mesh, in_specs=in_specs, out_specs=out_specs, check_vma=False)
```
